32 devices in a mesh: row: 4 (over x, core), col: 8 (over z, y).
Axes of the slice: x: 2, y: 2, z: 4, core: 2. Of those that a mesh axis runs over, the one named last changes fastest.
Arguments:
- activations: bfloat16 [64, 9216], P('row', 'col'), may hold values from -0.75 to 0.75
- cotangent: bfloat16 [64, 9216], P('col', 'row'), may hold values from -6 to 6
- weight: bfloat16 [9216, 9216], P('row', 'col'), may hold values from -0.0625 to 0.0625
- momentum: float32 [9216, 9216], P('row', 'col'), may hold values from -500 to 500
- right_factor: float32 [9216, 256], P('col'), may hold values from -6 to 6
Outputs:
- input_grad: bfloat16 [64, 9216], P('row', 'col')
- momentum_next: float32 [9216, 9216], P('row', 'col')
- right_next: float32 [9216, 256], P('col')
- weight_step: bfloat16 [9216, 9216], P('row', 'col')
The draws below stay inside these ranges and needn't reach their ends.
All inputs are finite; a program needn't handle non-finite values.
Results may differ from the reference program's by a relative error of at most 0.0011.
Values may be sent and summed in bfloat16 or wider, within the bound.
A program may use at most 128 MiB of HBM per device.

```python
import math
import jax
import jax.numpy as jnp
from jax import lax

DOUT = 9216
DIN = 9216
RANK = 256
TOKENS = 64


def draw_momentum(key, part):
    base_key, row_key, col_key = jax.random.split(jax.random.fold_in(key, 11), 3)
    values = jnp.clip(jax.random.normal(base_key, (DOUT, DIN), jnp.float32), -5.0, 5.0)
    half_span = 0.5 * math.log(10.0)
    row_scale = 3.0 ** (jnp.arange(DOUT, dtype=jnp.float32) / DOUT)
    row_scale = row_scale * jnp.exp(jax.random.uniform(row_key, (DOUT,), jnp.float32, -half_span, half_span))
    col_scale = 3.0 ** (jnp.arange(DIN, dtype=jnp.float32) / DIN)
    col_scale = col_scale * jnp.exp(jax.random.uniform(col_key, (DIN,), jnp.float32, -half_span, half_span))
    return (values * row_scale[:, None] * col_scale[None, :]).astype(jnp.float32)


def block_scale(rng, shape, shards, smallest, top_value):
    def one(position, shards_of):
        draws = jax.random.uniform(jax.random.fold_in(jax.random.fold_in(rng, 6), position), (shards_of,), jnp.float32, smallest / len(shards), top_value / len(shards))
        return jnp.repeat(jnp.exp(draws), shape[position] // shards_of).reshape((-1,) + (1,) * (len(shape) - position - 1))

    level = one(*shards[0])
    for cut in shards[1:]:
        level = level * one(*cut)
    return level


def noise(rng, extent, width, bound, shards=(), kind=jnp.bfloat16):
    array = jax.random.normal(rng, extent, jnp.float32) * width
    if len(shards) > 0:
        array = block_scale(rng, extent, shards, -0.22, 0.18) * array
    return jnp.clip(array, min=-bound, max=bound).astype(kind)


def setup_inputs(seed: int = 0) -> dict:
    seeds = jax.random.split(jax.random.key(seed), 6)
    return {
        "activations": noise(seeds[0], (TOKENS, DIN), TOKENS ** -0.5, 0.75, ((0, 4), (1, 8))),
        "cotangent": noise(seeds[1], (TOKENS, DOUT), 1.0, 6.0, ((0, 8), (1, 4))),
        "weight": noise(seeds[2], (DOUT, DIN), DOUT ** -0.5, 0.0625, ((0, 4), (1, 8))),
        "momentum": draw_momentum(jax.random.fold_in(seeds[5], 71), 0),
        "right_factor": noise(seeds[4], (DIN, RANK), 1.0, 6.0, ((0, 8),), jnp.float32),
    }


momentum_decay = 0.6
ridge_weight = 0.001

def reference(activations, cotangent, weight, momentum, right_factor):
    highest = lax.Precision.HIGHEST
    input_grad = jnp.dot(cotangent.astype(jnp.float32), weight.astype(jnp.float32), preferred_element_type=jnp.float32).astype(jnp.bfloat16)
    weight_grad = jnp.dot(cotangent.T.astype(jnp.float32), activations.astype(jnp.float32), preferred_element_type=jnp.float32)
    buffer = momentum + weight_grad
    left = jnp.dot(buffer, right_factor, precision=highest) / jnp.sqrt(jnp.float32(DIN))
    gram_matrix = jnp.dot(left.T, left, precision=highest) + ridge_weight * DOUT * jnp.eye(RANK, dtype=jnp.float32)
    factor_low = jnp.linalg.cholesky(gram_matrix)
    orthonormal = jax.scipy.linalg.solve_triangular(factor_low, left.T, lower=True).T
    right = jnp.dot(buffer.T, orthonormal, precision=highest)
    squares = lax.optimization_barrier(jnp.sum(right * right, axis=0))
    right_next = right * lax.rsqrt(squares / DIN + 1e-06)
    momentum_next = buffer - (1.0 - momentum_decay) * jnp.dot(orthonormal, right.T, precision=highest)
    step_scale = jnp.sqrt(jnp.float32(DOUT) / RANK)
    weight_step = (step_scale * jnp.dot(orthonormal, right_next.T, precision=highest)).astype(jnp.bfloat16)
    return (input_grad, momentum_next, right_next, weight_step)
```

```python
import functools

import jax
import jax.numpy as jnp
from jax import lax
from jax.experimental import pallas as pl
from jax.experimental.pallas import tpu as pltpu
from jax.sharding import PartitionSpec as P

momentum_decay = 0.6
ridge_weight = 0.001

HIGHEST = lax.Precision.HIGHEST
HIGH = lax.Precision.HIGH
SUBLANES = 8


def contract(left_side, right_side, left_dim, right_dim, precision):
    return lax.dot_general(
        left_side,
        right_side,
        (((left_dim,), (right_dim,)), ((), ())),
        precision=precision,
        preferred_element_type=jnp.float32,
    )


def identity(size):
    shape = (size, size)
    same = lax.broadcasted_iota(jnp.int32, shape, 0) == lax.broadcasted_iota(jnp.int32, shape, 1)
    return jnp.where(same, 1.0, 0.0).astype(jnp.float32)


def inverse_factor_kernel(block, ridge, gram_ref, inverse_ref, work, corner):
    size = gram_ref.shape[0]
    work[:, :size] = gram_ref[...] + ridge * identity(size)
    work[:, size:] = identity(size)
    row_in_group = lax.broadcasted_iota(jnp.int32, (SUBLANES, 2 * block), 0)
    for low in range(0, size, block):
        high = low + block
        corner[:, :block] = work[low:high, low:high]
        corner[:, block:] = identity(block)
        groups = [corner[g : g + SUBLANES, :] for g in range(0, block, SUBLANES)]
        for k in range(block):
            own, inside = divmod(k, SUBLANES)
            pivot_row = groups[own][inside : inside + 1, :]
            scaled = pivot_row / pivot_row[:, k : k + 1]
            for g in range(own, len(groups)):
                factor = groups[g][:, k : k + 1]
                change = factor * scaled
                if g == own:
                    change = jnp.where(row_in_group > inside, change, 0.0)
                groups[g] = groups[g] - change
        for g, rows in enumerate(groups):
            corner[g * SUBLANES : (g + 1) * SUBLANES, :] = rows
        pivots = jnp.sum(corner[:, :block] * identity(block), axis=1, keepdims=True)
        corner_inverse = corner[:, block:] * (1.0 / jnp.sqrt(pivots))
        panel = contract(corner_inverse, work[low:high, :], 1, 0, HIGHEST)
        inverse_ref[low:high, :] = panel[:, size:]
        if high < size:
            update = contract(panel[:, :size], panel, 0, 0, HIGHEST)
            work[high:, :] = work[high:, :] - update[high:, :]


def inverse_factor(gram_matrix, ridge):
    size = gram_matrix.shape[0]
    block = min(64, size)
    return pl.pallas_call(
        functools.partial(inverse_factor_kernel, block, ridge),
        out_shape=jax.ShapeDtypeStruct((size, size), jnp.float32),
        in_specs=[pl.BlockSpec(memory_space=pltpu.VMEM)],
        out_specs=pl.BlockSpec(memory_space=pltpu.VMEM),
        scratch_shapes=[
            pltpu.VMEM((size, 2 * size), jnp.float32),
            pltpu.VMEM((block, 2 * block), jnp.float32),
        ],
        cost_estimate=pl.CostEstimate(flops=20_000_000_000, bytes_accessed=8 * size * size, transcendentals=0),
        name="inverse_factor",
    )(gram_matrix)


def shards(rows_of, cols_of, activations, cotangent, weight, momentum, right_factor):
    dout = momentum.shape[0] * rows_of
    din = momentum.shape[1] * cols_of
    rank = right_factor.shape[1]
    cot_tokens = lax.all_gather(cotangent, "col", axis=0, tiled=True)
    act_tokens = lax.all_gather(activations, "row", axis=0, tiled=True)
    held_part = contract(momentum, right_factor, 1, 0, HIGH)
    act_part = contract(act_tokens.astype(jnp.float32), right_factor, 1, 0, HIGH)
    grad_part = contract(cot_tokens.astype(jnp.float32), act_part, 0, 0, HIGH)
    left_part = (held_part + grad_part) / jnp.sqrt(jnp.float32(din))
    left_piece = lax.psum_scatter(left_part, "col", scatter_dimension=0, tiled=True)
    input_part = jnp.dot(cot_tokens, weight, preferred_element_type=jnp.float32)
    buffer = momentum + contract(cot_tokens, act_tokens, 0, 0, None)
    left_block = lax.all_gather(left_piece, "col", axis=0, tiled=True)
    gram_matrix = lax.psum(contract(left_block, left_block, 0, 0, HIGHEST), "row")
    projected_part = contract(buffer, left_block, 0, 0, HIGH)
    gram_matrix, projected_part = lax.optimization_barrier((gram_matrix, projected_part))
    projected = lax.psum(projected_part, "row")
    projected, input_part = lax.optimization_barrier((projected, input_part))
    input_sums = lax.psum_scatter(input_part, "row", scatter_dimension=0, tiled=True)
    inverse = inverse_factor(gram_matrix, ridge_weight * dout)
    orthonormal = contract(left_block, inverse, 1, 1, HIGHEST)
    right = contract(projected, inverse, 1, 1, HIGHEST)
    squares = lax.psum(jnp.sum(right * right, axis=0), "col")
    momentum_next = buffer - (1.0 - momentum_decay) * contract(orthonormal, right, 1, 1, HIGH)
    right_next = right * lax.rsqrt(squares / din + 1e-06)
    step_scale = jnp.sqrt(jnp.float32(dout) / rank)
    weight_step = (step_scale * contract(orthonormal, right_next, 1, 1, HIGH)).astype(jnp.bfloat16)
    return (input_sums.astype(jnp.bfloat16), momentum_next, right_next, weight_step)


def solution(mesh):
    placed = (P("row", "col"), P("col", "row"), P("row", "col"), P("row", "col"), P("col", None))
    return jax.shard_map(
        functools.partial(shards, mesh.shape["row"], mesh.shape["col"]),
        mesh=mesh,
        in_specs=placed,
        out_specs=(P("row", "col"), P("row", "col"), P("col", None), P("row", "col")),
        check_vma=False,
    )
```
